32 devices in a mesh: seq: 8 (over y, x, core), dp: 4 (over z).
Axes of the slice: x: 2, y: 2, z: 4, core: 2. Of those that a mesh axis runs over, the one named last changes fastest.
Arguments:
- layer_input: bfloat16 [4, 1024, 5120], P('dp', 'seq'), may hold values from -64 to 64, as said below
- out_grad: bfloat16 [4, 1024, 5120], P('dp', 'seq'), may hold values from -0.059814453 to 0.059814453
- w_query: bfloat16 [5120, 640], replicated, may hold values from -0.078125 to 0.078125
- w_key: bfloat16 [5120, 128], replicated, may hold values from -0.078125 to 0.078125
- w_value: bfloat16 [5120, 128], replicated, may hold values from -0.078125 to 0.078125
- w_output: bfloat16 [640, 5120], replicated, may hold values from -0.25 to 0.25
- block_mask: int32 [4, 8, 8], P('dp'), may hold values from 0 to 1, as said below
Outputs:
- grad_qkv: float32 [5120, 896], P(('seq', 'dp'))
- grad_output: float32 [640, 5120], P(('seq', 'dp'))
The draws below stay inside these ranges and needn't reach their ends.
Inputs may be any that keep to these rules, and one draw needn't show every extreme that they name: `layer_input`: each position's entries are a bell-shaped or uniform body times a scale of that position; they may share a common direction, and some positions may repeat one strong vector. block_mask[r] has ones on its diagonal and zeros above it. The 8 blocks of sequence r form a shared prefix of at least half of them followed by a chosen branch and then a rejected branch, each of one block or more; a block attends every earlier or equal block of the prefix and of its own branch, and nothing else.
All inputs are finite; a program needn't handle non-finite values.
Results may differ from the reference program's by a relative error of at most 0.025.
The reference program's roundings to bfloat16 on the way (of `attn_grad`, `weights_b`, `attn_out`, `score_grad` and `query_grad`) count: a program that leaves them out, or rounds other values in their place, can miss the bound.
Values may be sent and summed in bfloat16 or wider, within the bound.
A program may use at most 128 MiB of HBM per device.

```python
import math
import jax
import jax.numpy as jnp
from jax import lax

D = 5120
HEAD = 128
GROUP = 5
BLOCK = 128
TOK_DEV = 128
LEN = 1024
ROWS = 4
N_SEQ = 8


def draw_layer_input(key, part):
    key_noise, key_scale = jax.random.split(key, 2)
    scales = jnp.exp(jax.random.uniform(key_scale, (ROWS, LEN, 1), jnp.float32, math.log(0.5), math.log(5.0)))
    values_all = jnp.clip(jax.random.normal(key_noise, (ROWS, LEN, D), jnp.float32), -12.0, 12.0) * scales
    return values_all.astype(jnp.bfloat16)


def draw_block_mask(key, part):
    blocks = LEN // BLOCK
    key_prefix, key_branch = jax.random.split(key)
    prefix_len = jax.random.randint(key_prefix, (ROWS, 1, 1), blocks // 2, blocks - 1)
    chosen_len = jax.random.randint(key_branch, (ROWS, 1, 1), 1, blocks - prefix_len)
    block_ids = jnp.arange(blocks, dtype=jnp.int32)
    query_ids = block_ids[None, :, None]
    key_ids = block_ids[None, None, :]
    query_seg = jnp.where(query_ids < prefix_len, 0, jnp.where(query_ids < prefix_len + chosen_len, 1, 2))
    key_seg = jnp.where(key_ids < prefix_len, 0, jnp.where(key_ids < prefix_len + chosen_len, 1, 2))
    allowed = (key_ids <= query_ids) & ((key_ids < prefix_len) | (query_seg == key_seg))
    return allowed.astype(jnp.int32)


def block_scale(rng, extent, shards, low, high):
    def one(dim, parts):
        steps = jax.random.uniform(jax.random.fold_in(jax.random.fold_in(rng, 6), dim), (parts,), jnp.float32, low / len(shards), high / len(shards))
        return jnp.repeat(jnp.exp(steps), extent[dim] // parts).reshape((-1,) + (1,) * (len(extent) - dim - 1))

    loudness = one(*shards[0])
    for cut in shards[1:]:
        loudness = loudness * one(*cut)
    return loudness


def scatter_about(key, dims, width, limit, cuts=(), kind=jnp.bfloat16):
    drawn = jax.random.normal(key, dims, jnp.float32) * width
    if len(cuts) > 0:
        drawn = block_scale(key, dims, cuts, -0.22, 0.18) * drawn
    return jnp.clip(drawn, min=-limit, max=limit).astype(kind)


def setup_inputs(seed: int = 0) -> dict:
    keys = jax.random.split(jax.random.key(seed), 8)
    layer_input = draw_layer_input(jax.random.fold_in(keys[7], 71), 0)
    out_grad = scatter_about(keys[1], (ROWS, LEN, D), 0.01, 0.059814453, ((0, 4), (1, 8)))
    w_query = scatter_about(keys[2], (D, GROUP * HEAD), D ** -0.5, 0.078125)
    w_key = scatter_about(keys[3], (D, HEAD), D ** -0.5, 0.078125)
    w_value = scatter_about(keys[4], (D, HEAD), D ** -0.5, 0.078125)
    w_output = scatter_about(keys[5], (GROUP * HEAD, D), (GROUP * HEAD) ** -0.5, 0.25)
    block_mask = draw_block_mask(jax.random.fold_in(keys[7], 71), 0)
    return dict(layer_input=layer_input, out_grad=out_grad, w_query=w_query, w_key=w_key, w_value=w_value, w_output=w_output, block_mask=block_mask)


def allowed_block(mask_table, first_row, row_count, length):
    query_pos = first_row + jnp.arange(row_count, dtype=jnp.int32)
    key_pos = jnp.arange(length, dtype=jnp.int32)
    mask_rows = lax.dynamic_slice_in_dim(mask_table, (first_row // BLOCK).astype(jnp.int32), row_count // BLOCK, 0)
    token_mask = jnp.repeat(jnp.repeat(mask_rows, BLOCK, axis=0), BLOCK, axis=1)
    same_block = query_pos[:, None] // BLOCK == key_pos[None, :] // BLOCK
    return (token_mask == 1) & (jnp.logical_not(same_block) | (key_pos[None, :] <= query_pos[:, None]))

def block_grads(queries, key_rows, value_rows, attn_grad, allowed, scale):
    query_wide = queries.astype(jnp.float32)
    key_wide = key_rows.astype(jnp.float32)
    value_wide = value_rows.astype(jnp.float32)
    grad_wide = attn_grad.astype(jnp.float32)
    scores = jnp.einsum('tgh,sh->gts', query_wide, key_wide) * scale
    masked = jnp.where(allowed[None], scores, -jnp.inf)
    row_max = lax.optimization_barrier(jnp.max(masked, axis=-1, keepdims=True))
    log_total = row_max + jnp.log(lax.optimization_barrier(jnp.sum(jnp.exp(masked - row_max), axis=-1, keepdims=True)))
    softmax_w = jnp.exp(masked - log_total)
    weights_b = softmax_w.astype(jnp.bfloat16)
    attn_out = jnp.einsum('gts,sh->tgh', weights_b.astype(jnp.float32), value_wide).astype(jnp.bfloat16)
    row_delta = jnp.einsum('tgh,tgh->gt', grad_wide, attn_out.astype(jnp.float32))
    prob_grad = jnp.einsum('tgh,sh->gts', grad_wide, value_wide)
    score_grad = (softmax_w * (prob_grad - row_delta[..., None])).astype(jnp.bfloat16)
    score_wide = score_grad.astype(jnp.float32)
    query_grad = (jnp.einsum('gts,sh->tgh', score_wide, key_wide) * scale).astype(jnp.bfloat16)
    key_grad = jnp.einsum('gts,tgh->sh', score_wide, query_wide) * scale
    value_grad = jnp.einsum('gts,tgh->sh', weights_b.astype(jnp.float32), grad_wide)
    return (attn_out, query_grad, key_grad, value_grad)

def reference(layer_input, out_grad, w_query, w_key, w_value, w_output, block_mask):
    scale = 1.0 / math.sqrt(HEAD)

    def row_grads(running, row_data):
        inputs_row, grad_row, mask_table = row_data
        queries = jnp.dot(inputs_row, w_query, preferred_element_type=jnp.float32).astype(jnp.bfloat16).reshape(LEN, GROUP, HEAD)
        key_rows = jnp.dot(inputs_row, w_key, preferred_element_type=jnp.float32).astype(jnp.bfloat16)
        value_rows = jnp.dot(inputs_row, w_value, preferred_element_type=jnp.float32).astype(jnp.bfloat16)
        attn_grad = jnp.dot(grad_row, w_output.T, preferred_element_type=jnp.float32).astype(jnp.bfloat16).reshape(LEN, GROUP, HEAD)

        def attend_block(key_accum, block_index):
            first_row = (block_index * TOK_DEV).astype(jnp.int32)
            query_block = lax.dynamic_slice_in_dim(queries, first_row, TOK_DEV, 0)
            grad_block = lax.dynamic_slice_in_dim(attn_grad, first_row, TOK_DEV, 0)
            allowed = allowed_block(mask_table, first_row, TOK_DEV, LEN)
            attn_out, query_grad, key_grad, value_grad = block_grads(query_block, key_rows, value_rows, grad_block, allowed, scale)
            return (key_accum + jnp.concatenate([key_grad, value_grad], axis=1), (attn_out, query_grad))
        key_accum, (attn_out, query_grad) = lax.scan(attend_block, jnp.zeros((LEN, 2 * HEAD), jnp.float32), jnp.arange(N_SEQ, dtype=jnp.int32))
        attn_out = attn_out.reshape(LEN, GROUP * HEAD)
        query_grad = query_grad.reshape(LEN, GROUP * HEAD)
        grads_all = jnp.concatenate([query_grad, key_accum.astype(jnp.bfloat16)], axis=1)
        qkv_term = jnp.dot(inputs_row.T, grads_all, preferred_element_type=jnp.float32)
        out_term = jnp.dot(attn_out.T, grad_row, preferred_element_type=jnp.float32)
        return ((running[0] + qkv_term, running[1] + out_term), None)
    zero_grads = (jnp.zeros((D, GROUP * HEAD + 2 * HEAD), jnp.float32), jnp.zeros((GROUP * HEAD, D), jnp.float32))
    totals, ignored = lax.scan(row_grads, zero_grads, (layer_input, out_grad, block_mask))
    return (totals[0], totals[1])
```

```python
import functools
import math

import jax
import jax.numpy as jnp
import ml_dtypes
import numpy as np
from jax import lax
from jax.experimental import pallas as pl
from jax.experimental.pallas import tpu as pltpu
from jax.sharding import PartitionSpec as P

F32 = jnp.float32
BF16 = jnp.bfloat16
MESH = pl.DeviceIdType.MESH
NT = (((1,), (1,)), ((), ()))
TN = (((0,), (0,)), ((), ()))


def round_up(value, step):
    return -(-value // step) * step


def head_row_selection(n_seq, n_dp, width):
    rows = width // (n_seq * n_dp)
    padded = round_up(rows, 8)
    chips = n_seq // 2
    table = np.zeros((width, 2, n_dp, chips, padded), np.float32)
    for core in range(2):
        for d in range(n_dp):
            for c in range(chips):
                for i in range(rows):
                    table[((c * 2 + core) * n_dp + d) * rows + i, core, d, c, i] = 1.0
    return table.reshape(width, -1).astype(ml_dtypes.bfloat16)


def kernel(
    n_seq, n_dp,
    x_ref, og_ref, wq_hbm, wk_hbm, wv_hbm, wo_hbm, mask_ref, sel_hbm,
    oqkv_ref, oout_ref,
    wq, wkv, wo, sel, xbuf, gbuf, kvall, kvsend, kvrecv, kvacc, abuf, qbuf, kgbuf,
    q3, d3, dt3, a3, qg3, kt, vt, bias,
    part_o, part_q, part_k,
    exo_s, exo_r, exq_s, exq_r, exk_s, exk_r,
    dpo_s, dpo_r, dpq_s, dpq_r, dpk_s, dpk_r, fo_s, fo_r,
    wsem, s_x, r_x, s_g, r_g, s_kv, r_kv, s_kr, r_kr, s_a, r_a, s_q, r_q, s_kg, r_kg,
    s_ex, r_ex, s_do, r_do, s_dq, r_dq, s_dk, r_dk, s_fo, r_fo,
):
    chips = n_seq // 2
    me = lax.axis_index("seq")
    md = lax.axis_index("dp")
    core = lax.rem(me, 2)
    chip = lax.div(me, 2)
    other = 1 - core
    tokens, depth = x_ref.shape
    heads, _, head = q3.shape
    width = depth // chips
    half = width // 2
    length = n_seq * tokens
    scale = 1.0 / math.sqrt(head)

    loads = [
        pltpu.make_async_copy(wk_hbm, wkv.at[:, 0:head], wsem.at[0]),
        pltpu.make_async_copy(wv_hbm, wkv.at[:, head : 2 * head], wsem.at[1]),
        pltpu.make_async_copy(wq_hbm, wq, wsem.at[2]),
        pltpu.make_async_copy(wo_hbm, wo, wsem.at[3]),
        pltpu.make_async_copy(sel_hbm, sel, wsem.at[4]),
    ]
    for load in loads:
        load.start()

    barrier = pltpu.get_barrier_semaphore()
    for k in range(1, n_seq):
        pl.semaphore_signal(
            barrier, inc=1, device_id={"seq": lax.rem(me + k, n_seq)}, device_id_type=MESH
        )
    for k in range(1, n_dp):
        pl.semaphore_signal(
            barrier, inc=1, device_id={"dp": lax.rem(md + k, n_dp)}, device_id_type=MESH
        )
    pl.semaphore_wait(barrier, n_seq + n_dp - 2)

    sent = []

    def spread(source, dest, slot, index, count, to_device, send_sems, recv_sems):
        copies = []
        for k in range(1, count):
            peer = lax.rem(index + k, count)
            copy = pltpu.make_async_remote_copy(
                src_ref=source(peer),
                dst_ref=dest.at[slot],
                send_sem=send_sems.at[k - 1],
                recv_sem=recv_sems.at[k - 1],
                device_id=to_device(peer),
                device_id_type=MESH,
            )
            copy.start()
            copies.append(copy)
        sent.extend(copies)
        return copies

    def to_seq(peer):
        return {"seq": peer}

    def to_chip(peer):
        return {"seq": peer * 2 + core}

    def to_dp(peer):
        return {"dp": peer}

    def over_chips(buf, send_sems, recv_sems):
        return spread(
            lambda peer: buf.at[chip], buf, chip, chip, chips, to_chip, send_sems, recv_sems
        )

    def swap(source, dest, i):
        copy = pltpu.make_async_remote_copy(
            src_ref=source, dst_ref=dest, send_sem=s_ex.at[i], recv_sem=r_ex.at[i],
            device_id={"seq": chip * 2 + other}, device_id_type=MESH,
        )
        copy.start()
        sent.append(copy)
        return copy

    def arrive(copies):
        for copy in copies:
            copy.wait_recv()

    def columns(index):
        return pl.ds(pl.multiple_of(index * width, 128), width)

    loads[0].wait()
    loads[1].wait()
    kvall[me] = jnp.dot(x_ref[...], wkv[...], preferred_element_type=F32).astype(BF16)
    got_kv = spread(lambda peer: kvall.at[me], kvall, me, me, n_seq, to_seq, s_kv, r_kv)

    got_g = spread(
        lambda peer: og_ref.at[:, columns(peer)], gbuf, chip, chip, chips, to_chip, s_g, r_g
    )
    got_x = spread(
        lambda peer: x_ref.at[:, columns(peer)], xbuf, chip, chip, chips, to_chip, s_x, r_x
    )
    xbuf[chip] = x_ref[:, columns(chip)]
    gbuf[chip] = og_ref[:, columns(chip)]

    loads[2].wait()
    queries = jnp.dot(x_ref[...], wq[...], preferred_element_type=F32)
    for g in range(heads):
        q3[g] = queries[:, g * head : (g + 1) * head].astype(BF16)
    loads[3].wait()
    for g in range(heads):
        grad_t = lax.dot_general(
            wo[g * head : (g + 1) * head, :], og_ref[...], NT, preferred_element_type=F32
        )
        dt3[g] = grad_t.astype(BF16)
        d3[g] = grad_t.T.astype(BF16)

    gap = lax.broadcasted_iota(jnp.int32, (tokens, tokens), 0) - lax.broadcasted_iota(
        jnp.int32, (tokens, tokens), 1
    )
    for j in range(n_seq):
        reach = jnp.where(mask_ref[me, j] == 1, jnp.where(me == j, 0, 4 * tokens), -4 * tokens)
        bias[j * tokens : (j + 1) * tokens, :] = jnp.where(gap <= reach, 0.0, -jnp.inf)

    kvacc[...] = jnp.zeros_like(kvacc)
    arrive(got_kv)
    for j in range(n_seq):
        rows = slice(j * tokens, (j + 1) * tokens)
        kt[:, rows] = kvall[j, :, 0:head].astype(F32).T.astype(BF16)
        vt[:, rows] = kvall[j, :, head : 2 * head].astype(F32).T.astype(BF16)

    @pl.loop(0, heads)
    def _(g):
        keys = kvall[:, :, 0:head].reshape(length, head)
        values = kvall[:, :, head : 2 * head].reshape(length, head)
        query = q3[g]
        grad_t = dt3[g]
        scores = lax.dot_general(keys, query, NT, preferred_element_type=F32) * scale + bias[...]
        top = jnp.max(scores, axis=0, keepdims=True)
        raised = jnp.exp(scores - top)
        probs = raised * (1.0 / jnp.sum(raised, axis=0, keepdims=True))
        weights = probs.astype(BF16)
        out_t = jnp.dot(vt[...], weights, preferred_element_type=F32).astype(BF16).astype(F32)
        delta = jnp.sum(grad_t.astype(F32) * out_t, axis=0, keepdims=True)
        prob_grad = jnp.dot(values, grad_t, preferred_element_type=F32)
        score_grad = (probs * (prob_grad - delta)).astype(BF16)
        a3[g] = out_t.T.astype(BF16)
        query_t = jnp.dot(kt[...], score_grad, preferred_element_type=F32) * scale
        qg3[g] = query_t.T.astype(BF16)
        kvacc[:, 0:head] += jnp.dot(score_grad, query, preferred_element_type=F32)
        kvacc[:, head : 2 * head] += jnp.dot(weights, d3[g], preferred_element_type=F32)

    loads[4].wait()
    attn = jnp.concatenate([a3[g] for g in range(heads)], axis=1)
    abuf[chip] = jnp.dot(attn, sel[...], preferred_element_type=F32).astype(BF16)
    got_a = over_chips(abuf, s_a, r_a)
    for j in range(n_seq):
        rows = slice(j * tokens, (j + 1) * tokens)
        kvsend[j, :, 0:head] = (kvacc[rows, 0:head] * scale).astype(BF16)
        kvsend[j, :, head : 2 * head] = kvacc[rows, head : 2 * head].astype(BF16)
    got_kr = spread(lambda peer: kvsend.at[peer], kvrecv, me, me, n_seq, to_seq, s_kr, r_kr)
    for g in range(heads):
        qbuf[chip, :, g * head : (g + 1) * head] = qg3[g]
    got_q = over_chips(qbuf, s_q, r_q)

    arrive(got_g)
    arrive(got_a)
    group = exo_s.shape[1]
    side = n_dp * group
    grads = gbuf[...].reshape(chips * tokens, width)

    def out_rows(which):
        picked = abuf[:, :, pl.ds(pl.multiple_of(which * side, 128), side)]
        return lax.dot_general(
            picked.reshape(chips * tokens, side), grads, TN, preferred_element_type=F32
        )

    theirs = out_rows(other)
    for d in range(n_dp):
        exo_s[d] = theirs[d * group : (d + 1) * group, :].astype(BF16)
    got_exo = swap(exo_s, exo_r, 0)
    part_o[...] = out_rows(core)

    arrive(got_kr)
    own = pl.ds(pl.multiple_of(me * tokens, tokens), tokens)
    key_sum = kvacc[own, 0:head] * scale
    value_sum = kvacc[own, head : 2 * head]
    for k in range(1, n_seq):
        peer = lax.rem(me + k, n_seq)
        key_sum += kvrecv[peer, :, 0:head].astype(F32)
        value_sum += kvrecv[peer, :, head : 2 * head].astype(F32)
    kgbuf[chip, :, 0:head] = key_sum.astype(BF16)
    kgbuf[chip, :, head : 2 * head] = value_sum.astype(BF16)
    got_kg = over_chips(kgbuf, s_kg, r_kg)

    got_exo.wait_recv()
    for d in range(n_dp):
        dpo_s[d] = (part_o[d * group : (d + 1) * group, :] + exo_r[d].astype(F32)).astype(BF16)
    got_do = spread(lambda peer: dpo_s.at[peer], dpo_r, md, md, n_dp, to_dp, s_do, r_do)

    owned = exq_s.shape[1]

    def rows_of(which, d):
        return pl.ds(pl.multiple_of(which * half + d * owned, 8), owned)

    def projection(grad_buf, part, ex_s, ex_r, i):
        features = xbuf[...].reshape(chips * tokens, width)
        grad = grad_buf[...].reshape(chips * tokens, grad_buf.shape[2])
        part[...] = lax.dot_general(features, grad, TN, preferred_element_type=F32)
        for d in range(n_dp):
            ex_s[d] = part[rows_of(other, d), :].astype(BF16)
        return swap(ex_s, ex_r, i)

    def reduce_dp(got_ex, part, ex_r, dp_s, dp_r, send_sems, recv_sems):
        got_ex.wait_recv()
        for d in range(n_dp):
            dp_s[d] = (part[rows_of(core, d), :] + ex_r[d].astype(F32)).astype(BF16)
        return spread(lambda peer: dp_s.at[peer], dp_r, md, md, n_dp, to_dp, send_sems, recv_sems)

    arrive(got_x)
    arrive(got_q)
    got_exq = projection(qbuf, part_q, exq_s, exq_r, 1)
    arrive(got_kg)
    got_dq = reduce_dp(got_exq, part_q, exq_r, dpq_s, dpq_r, s_dq, r_dq)
    got_exk = projection(kgbuf, part_k, exk_s, exk_r, 2)
    got_dk = reduce_dp(got_exk, part_k, exk_r, dpk_s, dpk_r, s_dk, r_dk)

    arrive(got_do)
    mine = pl.ds(pl.multiple_of(md * group, 8), group)
    total = part_o[mine, :] + exo_r[md].astype(F32)
    for k in range(1, n_dp):
        total += dpo_r[lax.rem(md + k, n_dp)].astype(F32)
    padded = group // chips
    for c in range(chips):
        fo_s[c] = total[c * padded : (c + 1) * padded, :].astype(BF16)
    got_fo = spread(lambda peer: fo_s.at[peer], fo_r, chip, chip, chips, to_chip, s_fo, r_fo)
    fo_r[chip] = fo_s[chip]

    def finish(part, ex_r, dp_r):
        result = part[rows_of(core, md), :] + ex_r[md].astype(F32)
        for k in range(1, n_dp):
            result += dp_r[lax.rem(md + k, n_dp)].astype(F32)
        return result

    q_columns = heads * head
    arrive(got_dq)
    oqkv_ref[:, 0:q_columns] = finish(part_q, exq_r, dpq_r)
    arrive(got_dk)
    oqkv_ref[:, q_columns:] = finish(part_k, exk_r, dpk_r)
    arrive(got_fo)
    for c in range(chips):
        oout_ref[:, c * width : (c + 1) * width] = fo_r[c].astype(F32)[0 : oout_ref.shape[0], :]
    for copy in sent:
        copy.wait_send()


def shards(n_seq, n_dp, layer_input, out_grad, w_query, w_key, w_value, w_output, block_mask):
    tokens, depth = layer_input.shape[1:]
    head = w_key.shape[1]
    q_width = w_query.shape[1]
    heads = q_width // head
    chips = n_seq // 2
    devices = n_seq * n_dp
    width = depth // chips
    rows_in = depth // devices
    rows_out = q_width // devices
    group = chips * round_up(rows_out, 8)
    side = n_dp * group
    length = n_seq * tokens
    selection = jnp.asarray(head_row_selection(n_seq, n_dp, q_width))
    vmem = pltpu.VMEM
    scratch = [
        vmem((depth, q_width), BF16), vmem((depth, 2 * head), BF16), vmem((q_width, depth), BF16),
        vmem((q_width, 2 * side), BF16),
        vmem((chips, tokens, width), BF16), vmem((chips, tokens, width), BF16),
        vmem((n_seq, tokens, 2 * head), BF16), vmem((n_seq, tokens, 2 * head), BF16),
        vmem((n_seq, tokens, 2 * head), BF16), vmem((length, 2 * head), F32),
        vmem((chips, tokens, 2 * side), BF16), vmem((chips, tokens, q_width), BF16),
        vmem((chips, tokens, 2 * head), BF16),
    ]
    scratch += [vmem((heads, tokens, head), BF16)] * 2 + [vmem((heads, head, tokens), BF16)]
    scratch += [vmem((heads, tokens, head), BF16)] * 2
    scratch += [vmem((head, length), BF16)] * 2 + [vmem((length, tokens), F32)]
    scratch += [vmem((side, width), F32), vmem((width, q_width), F32), vmem((width, 2 * head), F32)]
    out_block = vmem((n_dp, group, width), BF16)
    q_block = vmem((n_dp, rows_in, q_width), BF16)
    k_block = vmem((n_dp, rows_in, 2 * head), BF16)
    scratch += [out_block] * 2 + [q_block] * 2 + [k_block] * 2
    scratch += [out_block] * 2 + [q_block] * 2 + [k_block] * 2
    scratch += [vmem((chips, group // chips, width), BF16)] * 2
    dma = pltpu.SemaphoreType.DMA
    sems = [dma((5,))]
    for count in (chips, chips, n_seq, n_seq, chips, chips, chips, 4, n_dp, n_dp, n_dp, chips):
        sems += [dma((count - 1,))] * 2
    in_vmem = pl.BlockSpec(memory_space=pltpu.VMEM)
    in_hbm = pl.BlockSpec(memory_space=pl.ANY)
    return pl.pallas_call(
        functools.partial(kernel, n_seq, n_dp),
        out_shape=(
            jax.ShapeDtypeStruct((rows_in, q_width + 2 * head), F32),
            jax.ShapeDtypeStruct((rows_out, depth), F32),
        ),
        in_specs=[in_vmem, in_vmem, in_hbm, in_hbm, in_hbm, in_hbm,
                  pl.BlockSpec(memory_space=pltpu.SMEM), in_hbm],
        out_specs=(in_vmem, in_vmem),
        scratch_shapes=scratch + sems,
        compiler_params=pltpu.CompilerParams(
            collective_id=0, has_side_effects=True, vmem_limit_bytes=60 * 1024 * 1024
        ),
    )(layer_input[0], out_grad[0], w_query, w_key, w_value, w_output, block_mask[0], selection)


def solution(mesh):
    placed = (P("dp", "seq", None), P("dp", "seq", None), P(), P(), P(), P(), P("dp", None, None))
    return jax.shard_map(
        functools.partial(shards, mesh.shape["seq"], mesh.shape["dp"]),
        mesh=mesh,
        in_specs=placed,
        out_specs=(P(("seq", "dp"), None), P(("seq", "dp"), None)),
        check_vma=False,
    )
```

```python
import functools
import math

import jax
import jax.numpy as jnp
import ml_dtypes
import numpy as np
from jax import lax
from jax.experimental import pallas as pl
from jax.experimental.pallas import tpu as pltpu
from jax.sharding import PartitionSpec as P

F32 = jnp.float32
BF16 = jnp.bfloat16
MESH = pl.DeviceIdType.MESH
NT = (((1,), (1,)), ((), ()))
TN = (((0,), (0,)), ((), ()))


def round_up(value, step):
    return -(-value // step) * step


def head_row_selection(n_seq, n_dp, width):
    rows = width // (n_seq * n_dp)
    padded = round_up(rows, 8)
    chips = n_seq // 2
    table = np.zeros((width, 2, n_dp, chips, padded), np.float32)
    for core in range(2):
        for d in range(n_dp):
            for c in range(chips):
                for i in range(rows):
                    table[((c * 2 + core) * n_dp + d) * rows + i, core, d, c, i] = 1.0
    return table.reshape(width, -1).astype(ml_dtypes.bfloat16)


def kernel(
    n_seq, n_dp,
    x_hbm, og_hbm, wq_hbm, wk_hbm, wv_hbm, wo_hbm, mask_ref, sel_hbm,
    oqkv_ref, oout_ref,
    x_ref, og_ref, wq, wkv, wo, sel, xbuf, gbuf, kvall, kvsend, kvrecv, kvacc, abuf, qbuf, kgbuf,
    q3, d3, dt3, a3, qg3, kt, vt, bias,
    part_o, part_q, part_k,
    exo_s, exo_r, exq_s, exq_r, exk_s, exk_r,
    dpo_s, dpo_r, dpq_s, dpq_r, dpk_s, dpk_r, fo_s, fo_r,
    wsem, s_x, r_x, s_g, r_g, s_kv, r_kv, s_kr, r_kr, s_a, r_a, s_q, r_q, s_kg, r_kg,
    s_ex, r_ex, s_do, r_do, s_dq, r_dq, s_dk, r_dk, s_fo, r_fo,
):
    chips = n_seq // 2
    me = lax.axis_index("seq")
    md = lax.axis_index("dp")
    core = lax.rem(me, 2)
    chip = lax.div(me, 2)
    other = 1 - core
    tokens, depth = x_ref.shape
    heads, _, head = q3.shape
    width = depth // chips
    half = width // 2
    length = n_seq * tokens
    scale = 1.0 / math.sqrt(head)

    loads = [
        pltpu.make_async_copy(wk_hbm, wkv.at[:, 0:head], wsem.at[0]),
        pltpu.make_async_copy(wv_hbm, wkv.at[:, head : 2 * head], wsem.at[1]),
        pltpu.make_async_copy(x_hbm, x_ref, wsem.at[5]),
        pltpu.make_async_copy(og_hbm, og_ref, wsem.at[6]),
        pltpu.make_async_copy(wq_hbm, wq, wsem.at[2]),
        pltpu.make_async_copy(wo_hbm, wo, wsem.at[3]),
        pltpu.make_async_copy(sel_hbm, sel, wsem.at[4]),
    ]
    for load in loads:
        load.start()

    barrier = pltpu.get_barrier_semaphore()
    for k in range(1, n_seq):
        pl.semaphore_signal(
            barrier, inc=1, device_id={"seq": lax.rem(me + k, n_seq)}, device_id_type=MESH
        )
    for k in range(1, n_dp):
        pl.semaphore_signal(
            barrier, inc=1, device_id={"dp": lax.rem(md + k, n_dp)}, device_id_type=MESH
        )
    pl.semaphore_wait(barrier, n_seq + n_dp - 2)

    sent = []

    def spread(source, dest, slot, index, count, to_device, send_sems, recv_sems):
        copies = []
        for k in range(1, count):
            peer = lax.rem(index + k, count)
            copy = pltpu.make_async_remote_copy(
                src_ref=source(peer),
                dst_ref=dest.at[slot],
                send_sem=send_sems.at[k - 1],
                recv_sem=recv_sems.at[k - 1],
                device_id=to_device(peer),
                device_id_type=MESH,
            )
            copy.start()
            copies.append(copy)
        sent.extend(copies)
        return copies

    def to_seq(peer):
        return {"seq": peer}

    def to_chip(peer):
        return {"seq": peer * 2 + core}

    def to_dp(peer):
        return {"dp": peer}

    def over_chips(buf, send_sems, recv_sems):
        return spread(
            lambda peer: buf.at[chip], buf, chip, chip, chips, to_chip, send_sems, recv_sems
        )

    def swap(source, dest, i):
        copy = pltpu.make_async_remote_copy(
            src_ref=source, dst_ref=dest, send_sem=s_ex.at[i], recv_sem=r_ex.at[i],
            device_id={"seq": chip * 2 + other}, device_id_type=MESH,
        )
        copy.start()
        sent.append(copy)
        return copy

    def arrive(copies):
        for copy in copies:
            copy.wait_recv()

    def columns(index):
        return pl.ds(pl.multiple_of(index * width, 128), width)

    got_g = spread(
        lambda peer: og_hbm.at[:, columns(peer)], gbuf, chip, chip, chips, to_chip, s_g, r_g
    )

    loads[0].wait()
    loads[1].wait()
    loads[2].wait()
    kvall[me] = jnp.dot(x_ref[...], wkv[...], preferred_element_type=F32).astype(BF16)
    got_kv = spread(lambda peer: kvall.at[me], kvall, me, me, n_seq, to_seq, s_kv, r_kv)

    loads[3].wait()
    xbuf[chip] = x_ref[:, columns(chip)]
    gbuf[chip] = og_ref[:, columns(chip)]

    loads[4].wait()
    queries = jnp.dot(x_ref[...], wq[...], preferred_element_type=F32)
    for g in range(heads):
        q3[g] = queries[:, g * head : (g + 1) * head].astype(BF16)
    loads[5].wait()
    for g in range(heads):
        grad_t = lax.dot_general(
            wo[g * head : (g + 1) * head, :], og_ref[...], NT, preferred_element_type=F32
        )
        dt3[g] = grad_t.astype(BF16)
        d3[g] = grad_t.T.astype(BF16)

    gap = lax.broadcasted_iota(jnp.int32, (tokens, tokens), 0) - lax.broadcasted_iota(
        jnp.int32, (tokens, tokens), 1
    )
    for j in range(n_seq):
        reach = jnp.where(mask_ref[me, j] == 1, jnp.where(me == j, 0, 4 * tokens), -4 * tokens)
        bias[j * tokens : (j + 1) * tokens, :] = jnp.where(gap <= reach, 0.0, -jnp.inf)

    kvacc[...] = jnp.zeros_like(kvacc)
    arrive(got_kv)
    for j in range(n_seq):
        rows = slice(j * tokens, (j + 1) * tokens)
        kt[:, rows] = kvall[j, :, 0:head].astype(F32).T.astype(BF16)
        vt[:, rows] = kvall[j, :, head : 2 * head].astype(F32).T.astype(BF16)

    @pl.loop(0, heads)
    def _(g):
        keys = kvall[:, :, 0:head].reshape(length, head)
        values = kvall[:, :, head : 2 * head].reshape(length, head)
        query = q3[g]
        grad_t = dt3[g]
        scores = lax.dot_general(keys, query, NT, preferred_element_type=F32) * scale + bias[...]
        top = jnp.max(scores, axis=0, keepdims=True)
        raised = jnp.exp(scores - top)
        probs = raised * (1.0 / jnp.sum(raised, axis=0, keepdims=True))
        weights = probs.astype(BF16)
        out_t = jnp.dot(vt[...], weights, preferred_element_type=F32).astype(BF16).astype(F32)
        delta = jnp.sum(grad_t.astype(F32) * out_t, axis=0, keepdims=True)
        prob_grad = jnp.dot(values, grad_t, preferred_element_type=F32)
        score_grad = (probs * (prob_grad - delta)).astype(BF16)
        a3[g] = out_t.T.astype(BF16)
        query_t = jnp.dot(kt[...], score_grad, preferred_element_type=F32) * scale
        qg3[g] = query_t.T.astype(BF16)
        kvacc[:, 0:head] += jnp.dot(score_grad, query, preferred_element_type=F32)
        kvacc[:, head : 2 * head] += jnp.dot(weights, d3[g], preferred_element_type=F32)

    loads[6].wait()
    attn = jnp.concatenate([a3[g] for g in range(heads)], axis=1)
    abuf[chip] = jnp.dot(attn, sel[...], preferred_element_type=F32).astype(BF16)
    got_a = over_chips(abuf, s_a, r_a)
    for j in range(n_seq):
        rows = slice(j * tokens, (j + 1) * tokens)
        kvsend[j, :, 0:head] = (kvacc[rows, 0:head] * scale).astype(BF16)
        kvsend[j, :, head : 2 * head] = kvacc[rows, head : 2 * head].astype(BF16)
    for g in range(heads):
        qbuf[chip, :, g * head : (g + 1) * head] = qg3[g]

    arrive(got_g)
    arrive(got_a)
    got_kr = spread(lambda peer: kvsend.at[peer], kvrecv, me, me, n_seq, to_seq, s_kr, r_kr)
    got_x = spread(
        lambda peer: x_hbm.at[:, columns(peer)], xbuf, chip, chip, chips, to_chip, s_x, r_x
    )
    got_q = over_chips(qbuf, s_q, r_q)
    group = exo_s.shape[1]
    side = n_dp * group
    grads = gbuf[...].reshape(chips * tokens, width)

    def out_rows(which):
        picked = abuf[:, :, pl.ds(pl.multiple_of(which * side, 128), side)]
        return lax.dot_general(
            picked.reshape(chips * tokens, side), grads, TN, preferred_element_type=F32
        )

    theirs = out_rows(other)
    for d in range(n_dp):
        exo_s[d] = theirs[d * group : (d + 1) * group, :].astype(BF16)
    got_exo = swap(exo_s, exo_r, 0)
    part_o[...] = out_rows(core)

    got_exo.wait_recv()
    for d in range(n_dp):
        dpo_s[d] = (part_o[d * group : (d + 1) * group, :] + exo_r[d].astype(F32)).astype(BF16)
    got_do = spread(lambda peer: dpo_s.at[peer], dpo_r, md, md, n_dp, to_dp, s_do, r_do)

    arrive(got_kr)
    own = pl.ds(pl.multiple_of(me * tokens, tokens), tokens)
    key_sum = kvacc[own, 0:head] * scale
    value_sum = kvacc[own, head : 2 * head]
    for k in range(1, n_seq):
        peer = lax.rem(me + k, n_seq)
        key_sum += kvrecv[peer, :, 0:head].astype(F32)
        value_sum += kvrecv[peer, :, head : 2 * head].astype(F32)
    kgbuf[chip, :, 0:head] = key_sum.astype(BF16)
    kgbuf[chip, :, head : 2 * head] = value_sum.astype(BF16)
    got_kg = over_chips(kgbuf, s_kg, r_kg)

    owned = exq_s.shape[1]

    def rows_of(which, d):
        return pl.ds(pl.multiple_of(which * half + d * owned, 8), owned)

    def projection(grad_buf, part, ex_s, ex_r, i):
        features = xbuf[...].reshape(chips * tokens, width)
        grad = grad_buf[...].reshape(chips * tokens, grad_buf.shape[2])
        part[...] = lax.dot_general(features, grad, TN, preferred_element_type=F32)
        for d in range(n_dp):
            ex_s[d] = part[rows_of(other, d), :].astype(BF16)
        return swap(ex_s, ex_r, i)

    def reduce_dp(got_ex, part, ex_r, dp_s, dp_r, send_sems, recv_sems):
        got_ex.wait_recv()
        for d in range(n_dp):
            dp_s[d] = (part[rows_of(core, d), :] + ex_r[d].astype(F32)).astype(BF16)
        return spread(lambda peer: dp_s.at[peer], dp_r, md, md, n_dp, to_dp, send_sems, recv_sems)

    arrive(got_x)
    arrive(got_q)
    got_exq = projection(qbuf, part_q, exq_s, exq_r, 1)
    got_dq = reduce_dp(got_exq, part_q, exq_r, dpq_s, dpq_r, s_dq, r_dq)

    arrive(got_do)
    mine = pl.ds(pl.multiple_of(md * group, 8), group)
    total = part_o[mine, :] + exo_r[md].astype(F32)
    for k in range(1, n_dp):
        total += dpo_r[lax.rem(md + k, n_dp)].astype(F32)
    padded = group // chips
    for c in range(chips):
        fo_s[c] = total[c * padded : (c + 1) * padded, :].astype(BF16)
    got_fo = spread(lambda peer: fo_s.at[peer], fo_r, chip, chip, chips, to_chip, s_fo, r_fo)
    fo_r[chip] = fo_s[chip]

    arrive(got_kg)
    got_exk = projection(kgbuf, part_k, exk_s, exk_r, 2)
    got_dk = reduce_dp(got_exk, part_k, exk_r, dpk_s, dpk_r, s_dk, r_dk)

    def finish(part, ex_r, dp_r):
        result = part[rows_of(core, md), :] + ex_r[md].astype(F32)
        for k in range(1, n_dp):
            result += dp_r[lax.rem(md + k, n_dp)].astype(F32)
        return result

    q_columns = heads * head
    arrive(got_dq)
    oqkv_ref[:, 0:q_columns] = finish(part_q, exq_r, dpq_r)
    arrive(got_dk)
    oqkv_ref[:, q_columns:] = finish(part_k, exk_r, dpk_r)
    arrive(got_fo)
    for c in range(chips):
        oout_ref[:, c * width : (c + 1) * width] = fo_r[c].astype(F32)[0 : oout_ref.shape[0], :]
    for copy in sent:
        copy.wait_send()


def shards(n_seq, n_dp, layer_input, out_grad, w_query, w_key, w_value, w_output, block_mask):
    tokens, depth = layer_input.shape[1:]
    head = w_key.shape[1]
    q_width = w_query.shape[1]
    heads = q_width // head
    chips = n_seq // 2
    devices = n_seq * n_dp
    width = depth // chips
    rows_in = depth // devices
    rows_out = q_width // devices
    group = chips * round_up(rows_out, 8)
    side = n_dp * group
    length = n_seq * tokens
    selection = jnp.asarray(head_row_selection(n_seq, n_dp, q_width))
    vmem = pltpu.VMEM
    scratch = [
        vmem((tokens, depth), BF16), vmem((tokens, depth), BF16),
        vmem((depth, q_width), BF16), vmem((depth, 2 * head), BF16), vmem((q_width, depth), BF16),
        vmem((q_width, 2 * side), BF16),
        vmem((chips, tokens, width), BF16), vmem((chips, tokens, width), BF16),
        vmem((n_seq, tokens, 2 * head), BF16), vmem((n_seq, tokens, 2 * head), BF16),
        vmem((n_seq, tokens, 2 * head), BF16), vmem((length, 2 * head), F32),
        vmem((chips, tokens, 2 * side), BF16), vmem((chips, tokens, q_width), BF16),
        vmem((chips, tokens, 2 * head), BF16),
    ]
    scratch += [vmem((heads, tokens, head), BF16)] * 2 + [vmem((heads, head, tokens), BF16)]
    scratch += [vmem((heads, tokens, head), BF16)] * 2
    scratch += [vmem((head, length), BF16)] * 2 + [vmem((length, tokens), F32)]
    scratch += [vmem((side, width), F32), vmem((width, q_width), F32), vmem((width, 2 * head), F32)]
    out_block = vmem((n_dp, group, width), BF16)
    q_block = vmem((n_dp, rows_in, q_width), BF16)
    k_block = vmem((n_dp, rows_in, 2 * head), BF16)
    scratch += [out_block] * 2 + [q_block] * 2 + [k_block] * 2
    scratch += [out_block] * 2 + [q_block] * 2 + [k_block] * 2
    scratch += [vmem((chips, group // chips, width), BF16)] * 2
    dma = pltpu.SemaphoreType.DMA
    sems = [dma((7,))]
    for count in (chips, chips, n_seq, n_seq, chips, chips, chips, 4, n_dp, n_dp, n_dp, chips):
        sems += [dma((count - 1,))] * 2
    in_vmem = pl.BlockSpec(memory_space=pltpu.VMEM)
    in_hbm = pl.BlockSpec(memory_space=pl.ANY)
    return pl.pallas_call(
        functools.partial(kernel, n_seq, n_dp),
        out_shape=(
            jax.ShapeDtypeStruct((rows_in, q_width + 2 * head), F32),
            jax.ShapeDtypeStruct((rows_out, depth), F32),
        ),
        in_specs=[in_hbm, in_hbm, in_hbm, in_hbm, in_hbm, in_hbm,
                  pl.BlockSpec(memory_space=pltpu.SMEM), in_hbm],
        out_specs=(in_vmem, in_vmem),
        scratch_shapes=scratch + sems,
        compiler_params=pltpu.CompilerParams(
            collective_id=0, has_side_effects=True, vmem_limit_bytes=60 * 1024 * 1024
        ),
    )(layer_input[0], out_grad[0], w_query, w_key, w_value, w_output, block_mask[0], selection)


def solution(mesh):
    placed = (P("dp", "seq", None), P("dp", "seq", None), P(), P(), P(), P(), P("dp", None, None))
    return jax.shard_map(
        functools.partial(shards, mesh.shape["seq"], mesh.shape["dp"]),
        mesh=mesh,
        in_specs=placed,
        out_specs=(P(("seq", "dp"), None), P(("seq", "dp"), None)),
        check_vma=False,
    )
```

```python
import functools
import math

import jax
import jax.numpy as jnp
import ml_dtypes
import numpy as np
from jax import lax
from jax.experimental import pallas as pl
from jax.experimental.pallas import tpu as pltpu
from jax.sharding import PartitionSpec as P

F32 = jnp.float32
BF16 = jnp.bfloat16
MESH = pl.DeviceIdType.MESH
NT = (((1,), (1,)), ((), ()))
TN = (((0,), (0,)), ((), ()))


def round_up(value, step):
    return -(-value // step) * step


def head_row_selection(n_seq, n_dp, width):
    rows = width // (n_seq * n_dp)
    padded = round_up(rows, 8)
    chips = n_seq // 2
    table = np.zeros((width, 2, n_dp, chips, padded), np.float32)
    for core in range(2):
        for d in range(n_dp):
            for c in range(chips):
                for i in range(rows):
                    table[((c * 2 + core) * n_dp + d) * rows + i, core, d, c, i] = 1.0
    return table.reshape(width, -1).astype(ml_dtypes.bfloat16)


def kernel(
    n_seq, n_dp,
    x_hbm, og_hbm, wq_hbm, wk_hbm, wv_hbm, wo_hbm, mask_ref, sel_hbm,
    oqkv_ref, oout_ref,
    x_ref, og_ref, wq, wkv, wo, sel, xbuf, gbuf, kvall, kvsend, kvrecv, kvpair, kvacc, abuf, qbuf, kgbuf,
    q3, d3, dt3, a3, qg3, kt, vt, bias,
    part_o, part_q, part_k,
    exo_s, exo_r, exq_s, exq_r, exk_s, exk_r,
    dpo_s, dpo_r, dpq_s, dpq_r, dpk_s, dpk_r, fo_s, fo_r,
    wsem, s_x, r_x, s_g, r_g, s_kv, r_kv, s_kr, r_kr, s_a, r_a, s_q, r_q, s_kg, r_kg,
    s_ex, r_ex, s_do, r_do, s_dq, r_dq, s_dk, r_dk, s_fo, r_fo,
):
    chips = n_seq // 2
    me = lax.axis_index("seq")
    md = lax.axis_index("dp")
    core = lax.rem(me, 2)
    chip = lax.div(me, 2)
    other = 1 - core
    tokens, depth = x_ref.shape
    heads, _, head = q3.shape
    width = depth // chips
    half = width // 2
    length = n_seq * tokens
    scale = 1.0 / math.sqrt(head)

    loads = [
        pltpu.make_async_copy(wk_hbm, wkv.at[:, 0:head], wsem.at[0]),
        pltpu.make_async_copy(wv_hbm, wkv.at[:, head : 2 * head], wsem.at[1]),
        pltpu.make_async_copy(x_hbm, x_ref, wsem.at[5]),
        pltpu.make_async_copy(og_hbm, og_ref, wsem.at[6]),
        pltpu.make_async_copy(wq_hbm, wq, wsem.at[2]),
        pltpu.make_async_copy(wo_hbm, wo, wsem.at[3]),
        pltpu.make_async_copy(sel_hbm, sel, wsem.at[4]),
    ]
    for load in loads:
        load.start()

    barrier = pltpu.get_barrier_semaphore()
    for k in range(1, n_seq):
        pl.semaphore_signal(
            barrier, inc=1, device_id={"seq": lax.rem(me + k, n_seq)}, device_id_type=MESH
        )
    for k in range(1, n_dp):
        pl.semaphore_signal(
            barrier, inc=1, device_id={"dp": lax.rem(md + k, n_dp)}, device_id_type=MESH
        )
    pl.semaphore_wait(barrier, n_seq + n_dp - 2)

    sent = []

    def spread(source, dest, slot, index, count, to_device, send_sems, recv_sems):
        copies = []
        for k in range(1, count):
            peer = lax.rem(index + k, count)
            copy = pltpu.make_async_remote_copy(
                src_ref=source(peer),
                dst_ref=dest.at[slot],
                send_sem=send_sems.at[k - 1],
                recv_sem=recv_sems.at[k - 1],
                device_id=to_device(peer),
                device_id_type=MESH,
            )
            copy.start()
            copies.append(copy)
        sent.extend(copies)
        return copies

    def to_chip(peer):
        return {"seq": peer * 2 + core}

    def to_dp(peer):
        return {"dp": peer}

    def over_chips(buf, send_sems, recv_sems):
        return spread(
            lambda peer: buf.at[chip], buf, chip, chip, chips, to_chip, send_sems, recv_sems
        )

    def swap(source, dest, i):
        copy = pltpu.make_async_remote_copy(
            src_ref=source, dst_ref=dest, send_sem=s_ex.at[i], recv_sem=r_ex.at[i],
            device_id={"seq": chip * 2 + other}, device_id_type=MESH,
        )
        copy.start()
        sent.append(copy)
        return copy

    def arrive(copies):
        for copy in copies:
            copy.wait_recv()

    def columns(index):
        return pl.ds(pl.multiple_of(index * width, 128), width)

    loads[0].wait()
    loads[1].wait()
    loads[2].wait()
    kvall[me] = jnp.dot(x_ref[...], wkv[...], preferred_element_type=F32).astype(BF16)
    got_kv = spread(lambda peer: kvall.at[me], kvall, me, chip, chips, to_chip, s_kv, r_kv)

    def to_other(source, dest, send_sems, recv_sems, i):
        copy = pltpu.make_async_remote_copy(
            src_ref=source, dst_ref=dest, send_sem=send_sems.at[i], recv_sem=recv_sems.at[i],
            device_id={"seq": chip * 2 + other}, device_id_type=MESH,
        )
        copy.start()
        sent.append(copy)
        return copy

    got_pair = [to_other(kvall.at[me], kvall.at[me], s_kv, r_kv, chips - 1)]

    got_g = spread(
        lambda peer: og_hbm.at[:, columns(peer)], gbuf, chip, chip, chips, to_chip, s_g, r_g
    )

    loads[3].wait()
    xbuf[chip] = x_ref[:, columns(chip)]
    gbuf[chip] = og_ref[:, columns(chip)]

    loads[4].wait()
    queries = jnp.dot(x_ref[...], wq[...], preferred_element_type=F32)
    for g in range(heads):
        q3[g] = queries[:, g * head : (g + 1) * head].astype(BF16)
    for k in range(1, chips):
        got_kv[k - 1].wait_recv()
        block = kvall.at[lax.rem(chip + chips - k, chips) * 2 + core]
        got_pair.append(to_other(block, block, s_kv, r_kv, chips - 1 + k))

    loads[5].wait()
    for g in range(heads):
        grad_t = lax.dot_general(
            wo[g * head : (g + 1) * head, :], og_ref[...], NT, preferred_element_type=F32
        )
        dt3[g] = grad_t.astype(BF16)
        d3[g] = grad_t.T.astype(BF16)

    gap = lax.broadcasted_iota(jnp.int32, (tokens, tokens), 0) - lax.broadcasted_iota(
        jnp.int32, (tokens, tokens), 1
    )
    for j in range(n_seq):
        reach = jnp.where(mask_ref[me, j] == 1, jnp.where(me == j, 0, 4 * tokens), -4 * tokens)
        bias[j * tokens : (j + 1) * tokens, :] = jnp.where(gap <= reach, 0.0, -jnp.inf)

    kvacc[...] = jnp.zeros_like(kvacc)
    arrive(got_pair)
    for j in range(n_seq):
        rows = slice(j * tokens, (j + 1) * tokens)
        kt[:, rows] = kvall[j, :, 0:head].astype(F32).T.astype(BF16)
        vt[:, rows] = kvall[j, :, head : 2 * head].astype(F32).T.astype(BF16)

    @pl.loop(0, heads)
    def _(g):
        keys = kvall[:, :, 0:head].reshape(length, head)
        values = kvall[:, :, head : 2 * head].reshape(length, head)
        query = q3[g]
        grad_t = dt3[g]
        scores = lax.dot_general(keys, query, NT, preferred_element_type=F32) * scale + bias[...]
        top = jnp.max(scores, axis=0, keepdims=True)
        raised = jnp.exp(scores - top)
        probs = raised * (1.0 / jnp.sum(raised, axis=0, keepdims=True))
        weights = probs.astype(BF16)
        out_t = jnp.dot(vt[...], weights, preferred_element_type=F32).astype(BF16).astype(F32)
        delta = jnp.sum(grad_t.astype(F32) * out_t, axis=0, keepdims=True)
        prob_grad = jnp.dot(values, grad_t, preferred_element_type=F32)
        score_grad = (probs * (prob_grad - delta)).astype(BF16)
        a3[g] = out_t.T.astype(BF16)
        query_t = jnp.dot(kt[...], score_grad, preferred_element_type=F32) * scale
        qg3[g] = query_t.T.astype(BF16)
        kvacc[:, 0:head] += jnp.dot(score_grad, query, preferred_element_type=F32)
        kvacc[:, head : 2 * head] += jnp.dot(weights, d3[g], preferred_element_type=F32)

    loads[6].wait()
    attn = jnp.concatenate([a3[g] for g in range(heads)], axis=1)
    abuf[chip] = jnp.dot(attn, sel[...], preferred_element_type=F32).astype(BF16)
    got_a = over_chips(abuf, s_a, r_a)
    for j in range(n_seq):
        rows = slice(j * tokens, (j + 1) * tokens)
        kvsend[j % 2, j // 2, :, 0:head] = (kvacc[rows, 0:head] * scale).astype(BF16)
        kvsend[j % 2, j // 2, :, head : 2 * head] = kvacc[rows, head : 2 * head].astype(BF16)
    got_kx = to_other(kvsend.at[other], kvrecv.at[pl.ds(0, chips)], s_kr, r_kr, chips - 1)
    for g in range(heads):
        qbuf[chip, :, g * head : (g + 1) * head] = qg3[g]

    arrive(got_g)
    arrive(got_a)
    got_kx.wait_recv()
    for c in range(chips):
        rows = pl.ds(pl.multiple_of((c * 2 + core) * tokens, tokens), tokens)
        key_pair = kvacc[rows, 0:head] * scale + kvrecv[c, :, 0:head].astype(F32)
        value_pair = kvacc[rows, head : 2 * head] + kvrecv[c, :, head : 2 * head].astype(F32)
        kvpair[c, :, 0:head] = key_pair.astype(BF16)
        kvpair[c, :, head : 2 * head] = value_pair.astype(BF16)
    got_kr = spread(
        lambda peer: kvpair.at[peer], kvrecv, chips + chip, chip, chips, to_chip, s_kr, r_kr
    )
    got_x = spread(
        lambda peer: x_hbm.at[:, columns(peer)], xbuf, chip, chip, chips, to_chip, s_x, r_x
    )
    got_q = over_chips(qbuf, s_q, r_q)
    group = exo_s.shape[1]
    side = n_dp * group
    grads = gbuf[...].reshape(chips * tokens, width)

    def out_rows(which):
        picked = abuf[:, :, pl.ds(pl.multiple_of(which * side, 128), side)]
        return lax.dot_general(
            picked.reshape(chips * tokens, side), grads, TN, preferred_element_type=F32
        )

    theirs = out_rows(other)
    for d in range(n_dp):
        exo_s[d] = theirs[d * group : (d + 1) * group, :].astype(BF16)
    got_exo = swap(exo_s, exo_r, 0)
    part_o[...] = out_rows(core)

    got_exo.wait_recv()
    for d in range(n_dp):
        dpo_s[d] = (part_o[d * group : (d + 1) * group, :] + exo_r[d].astype(F32)).astype(BF16)
    got_do = spread(lambda peer: dpo_s.at[peer], dpo_r, md, md, n_dp, to_dp, s_do, r_do)

    arrive(got_kr)
    own = pl.ds(pl.multiple_of(me * tokens, tokens), tokens)
    key_sum = kvacc[own, 0:head] * scale + kvrecv[chip, :, 0:head].astype(F32)
    value_sum = kvacc[own, head : 2 * head] + kvrecv[chip, :, head : 2 * head].astype(F32)
    for k in range(1, chips):
        peer = chips + lax.rem(chip + k, chips)
        key_sum += kvrecv[peer, :, 0:head].astype(F32)
        value_sum += kvrecv[peer, :, head : 2 * head].astype(F32)
    kgbuf[chip, :, 0:head] = key_sum.astype(BF16)
    kgbuf[chip, :, head : 2 * head] = value_sum.astype(BF16)
    got_kg = over_chips(kgbuf, s_kg, r_kg)

    owned = exq_s.shape[1]

    def rows_of(which, d):
        return pl.ds(pl.multiple_of(which * half + d * owned, 8), owned)

    def projection(grad_buf, part, ex_s, ex_r, i):
        features = xbuf[...].reshape(chips * tokens, width)
        grad = grad_buf[...].reshape(chips * tokens, grad_buf.shape[2])
        part[...] = lax.dot_general(features, grad, TN, preferred_element_type=F32)
        for d in range(n_dp):
            ex_s[d] = part[rows_of(other, d), :].astype(BF16)
        return swap(ex_s, ex_r, i)

    def reduce_dp(got_ex, part, ex_r, dp_s, dp_r, send_sems, recv_sems):
        got_ex.wait_recv()
        for d in range(n_dp):
            dp_s[d] = (part[rows_of(core, d), :] + ex_r[d].astype(F32)).astype(BF16)
        return spread(lambda peer: dp_s.at[peer], dp_r, md, md, n_dp, to_dp, send_sems, recv_sems)

    arrive(got_x)
    arrive(got_q)
    got_exq = projection(qbuf, part_q, exq_s, exq_r, 1)
    got_dq = reduce_dp(got_exq, part_q, exq_r, dpq_s, dpq_r, s_dq, r_dq)

    arrive(got_do)
    mine = pl.ds(pl.multiple_of(md * group, 8), group)
    total = part_o[mine, :] + exo_r[md].astype(F32)
    for k in range(1, n_dp):
        total += dpo_r[lax.rem(md + k, n_dp)].astype(F32)
    padded = group // chips
    for c in range(chips):
        fo_s[c] = total[c * padded : (c + 1) * padded, :].astype(BF16)
    got_fo = spread(lambda peer: fo_s.at[peer], fo_r, chip, chip, chips, to_chip, s_fo, r_fo)
    fo_r[chip] = fo_s[chip]

    arrive(got_kg)
    got_exk = projection(kgbuf, part_k, exk_s, exk_r, 2)
    got_dk = reduce_dp(got_exk, part_k, exk_r, dpk_s, dpk_r, s_dk, r_dk)

    def finish(part, ex_r, dp_r):
        result = part[rows_of(core, md), :] + ex_r[md].astype(F32)
        for k in range(1, n_dp):
            result += dp_r[lax.rem(md + k, n_dp)].astype(F32)
        return result

    q_columns = heads * head
    arrive(got_dq)
    oqkv_ref[:, 0:q_columns] = finish(part_q, exq_r, dpq_r)
    arrive(got_dk)
    oqkv_ref[:, q_columns:] = finish(part_k, exk_r, dpk_r)
    arrive(got_fo)
    for c in range(chips):
        oout_ref[:, c * width : (c + 1) * width] = fo_r[c].astype(F32)[0 : oout_ref.shape[0], :]
    for copy in sent:
        copy.wait_send()


def shards(n_seq, n_dp, layer_input, out_grad, w_query, w_key, w_value, w_output, block_mask):
    tokens, depth = layer_input.shape[1:]
    head = w_key.shape[1]
    q_width = w_query.shape[1]
    heads = q_width // head
    chips = n_seq // 2
    devices = n_seq * n_dp
    width = depth // chips
    rows_in = depth // devices
    rows_out = q_width // devices
    group = chips * round_up(rows_out, 8)
    side = n_dp * group
    length = n_seq * tokens
    selection = jnp.asarray(head_row_selection(n_seq, n_dp, q_width))
    vmem = pltpu.VMEM
    scratch = [
        vmem((tokens, depth), BF16), vmem((tokens, depth), BF16),
        vmem((depth, q_width), BF16), vmem((depth, 2 * head), BF16), vmem((q_width, depth), BF16),
        vmem((q_width, 2 * side), BF16),
        vmem((chips, tokens, width), BF16), vmem((chips, tokens, width), BF16),
        vmem((n_seq, tokens, 2 * head), BF16), vmem((2, chips, tokens, 2 * head), BF16),
        vmem((n_seq, tokens, 2 * head), BF16), vmem((chips, tokens, 2 * head), BF16),
        vmem((length, 2 * head), F32),
        vmem((chips, tokens, 2 * side), BF16), vmem((chips, tokens, q_width), BF16),
        vmem((chips, tokens, 2 * head), BF16),
    ]
    scratch += [vmem((heads, tokens, head), BF16)] * 2 + [vmem((heads, head, tokens), BF16)]
    scratch += [vmem((heads, tokens, head), BF16)] * 2
    scratch += [vmem((head, length), BF16)] * 2 + [vmem((length, tokens), F32)]
    scratch += [vmem((side, width), F32), vmem((width, q_width), F32), vmem((width, 2 * head), F32)]
    out_block = vmem((n_dp, group, width), BF16)
    q_block = vmem((n_dp, rows_in, q_width), BF16)
    k_block = vmem((n_dp, rows_in, 2 * head), BF16)
    scratch += [out_block] * 2 + [q_block] * 2 + [k_block] * 2
    scratch += [out_block] * 2 + [q_block] * 2 + [k_block] * 2
    scratch += [vmem((chips, group // chips, width), BF16)] * 2
    dma = pltpu.SemaphoreType.DMA
    sems = [dma((7,))]
    for count in (chips, chips, n_seq, n_seq, chips, chips, chips, 4, n_dp, n_dp, n_dp, chips):
        sems += [dma((count - 1,))] * 2
    in_vmem = pl.BlockSpec(memory_space=pltpu.VMEM)
    in_hbm = pl.BlockSpec(memory_space=pl.ANY)
    return pl.pallas_call(
        functools.partial(kernel, n_seq, n_dp),
        out_shape=(
            jax.ShapeDtypeStruct((rows_in, q_width + 2 * head), F32),
            jax.ShapeDtypeStruct((rows_out, depth), F32),
        ),
        in_specs=[in_hbm, in_hbm, in_hbm, in_hbm, in_hbm, in_hbm,
                  pl.BlockSpec(memory_space=pltpu.SMEM), in_hbm],
        out_specs=(in_vmem, in_vmem),
        scratch_shapes=scratch + sems,
        compiler_params=pltpu.CompilerParams(
            collective_id=0, has_side_effects=True, vmem_limit_bytes=60 * 1024 * 1024
        ),
    )(layer_input[0], out_grad[0], w_query, w_key, w_value, w_output, block_mask[0], selection)


def solution(mesh):
    placed = (P("dp", "seq", None), P("dp", "seq", None), P(), P(), P(), P(), P("dp", None, None))
    return jax.shard_map(
        functools.partial(shards, mesh.shape["seq"], mesh.shape["dp"]),
        mesh=mesh,
        in_specs=placed,
        out_specs=(P(("seq", "dp"), None), P(("seq", "dp"), None)),
        check_vma=False,
    )
```

```python
import functools
import math

import jax
import jax.numpy as jnp
import ml_dtypes
import numpy as np
from jax import lax
from jax.experimental import pallas as pl
from jax.experimental.pallas import tpu as pltpu
from jax.sharding import PartitionSpec as P

F32 = jnp.float32
BF16 = jnp.bfloat16
MESH = pl.DeviceIdType.MESH
NT = (((1,), (1,)), ((), ()))
TN = (((0,), (0,)), ((), ()))


def round_up(value, step):
    return -(-value // step) * step


def head_row_selection(n_seq, n_dp, width):
    rows = width // (n_seq * n_dp)
    padded = round_up(rows, 8)
    chips = n_seq // 2
    table = np.zeros((width, 2, n_dp, chips, padded), np.float32)
    for core in range(2):
        for d in range(n_dp):
            for c in range(chips):
                for i in range(rows):
                    table[((c * 2 + core) * n_dp + d) * rows + i, core, d, c, i] = 1.0
    return table.reshape(width, -1).astype(ml_dtypes.bfloat16)


def kernel(
    n_seq, n_dp,
    x_hbm, og_hbm, wq_hbm, wk_hbm, wv_hbm, wo_hbm, mask_ref, sel_hbm,
    oqkv_ref, oout_ref,
    x_ref, og_ref, wq, wkv, wo, sel, xbuf, gbuf, kvall, kvsend, kvrecv, kvpair, kvacc, abuf, qbuf, kgbuf,
    q3, d3, dt3, a3, qg3, kt, vt, bias,
    part_o, part_q, part_k,
    exo_s, exo_r, exq_s, exq_r, exk_s, exk_r,
    dpo_s, dpo_r, dpq_s, dpq_r, dpk_s, dpk_r, fo_s, fo_r,
    wsem, s_x, r_x, s_g, r_g, s_kv, r_kv, s_kr, r_kr, s_a, r_a, s_q, r_q, s_kg, r_kg,
    s_ex, r_ex, s_do, r_do, s_dq, r_dq, s_dk, r_dk, s_fo, r_fo,
):
    chips = n_seq // 2
    me = lax.axis_index("seq")
    md = lax.axis_index("dp")
    core = lax.rem(me, 2)
    chip = lax.div(me, 2)
    other = 1 - core
    tokens, depth = x_ref.shape
    heads, _, head = q3.shape
    width = depth // chips
    half = width // 2
    length = n_seq * tokens
    scale = 1.0 / math.sqrt(head)

    loads = [
        pltpu.make_async_copy(wk_hbm, wkv.at[:, 0:head], wsem.at[0]),
        pltpu.make_async_copy(wv_hbm, wkv.at[:, head : 2 * head], wsem.at[1]),
        pltpu.make_async_copy(x_hbm, x_ref, wsem.at[5]),
        pltpu.make_async_copy(og_hbm, og_ref, wsem.at[6]),
        pltpu.make_async_copy(wq_hbm, wq, wsem.at[2]),
        pltpu.make_async_copy(wo_hbm, wo, wsem.at[3]),
        pltpu.make_async_copy(sel_hbm, sel, wsem.at[4]),
    ]
    for load in loads:
        load.start()

    barrier = pltpu.get_barrier_semaphore()
    for k in range(1, n_seq):
        pl.semaphore_signal(
            barrier, inc=1, device_id={"seq": lax.rem(me + k, n_seq)}, device_id_type=MESH
        )
    for k in range(1, n_dp):
        pl.semaphore_signal(
            barrier, inc=1, device_id={"dp": lax.rem(md + k, n_dp)}, device_id_type=MESH
        )
    pl.semaphore_wait(barrier, n_seq + n_dp - 2)

    sent = []

    def spread(source, dest, slot, index, count, to_device, send_sems, recv_sems):
        copies = []
        for k in range(1, count):
            peer = lax.rem(index + k, count)
            copy = pltpu.make_async_remote_copy(
                src_ref=source(peer),
                dst_ref=dest.at[slot],
                send_sem=send_sems.at[k - 1],
                recv_sem=recv_sems.at[k - 1],
                device_id=to_device(peer),
                device_id_type=MESH,
            )
            copy.start()
            copies.append(copy)
        sent.extend(copies)
        return copies

    def to_chip(peer):
        return {"seq": peer * 2 + core}

    def to_dp(peer):
        return {"dp": peer}

    def over_chips(buf, send_sems, recv_sems):
        return spread(
            lambda peer: buf.at[chip], buf, chip, chip, chips, to_chip, send_sems, recv_sems
        )

    def swap(source, dest, i):
        copy = pltpu.make_async_remote_copy(
            src_ref=source, dst_ref=dest, send_sem=s_ex.at[i], recv_sem=r_ex.at[i],
            device_id={"seq": chip * 2 + other}, device_id_type=MESH,
        )
        copy.start()
        sent.append(copy)
        return copy

    def arrive(copies):
        for copy in copies:
            copy.wait_recv()

    def columns(index):
        return pl.ds(pl.multiple_of(index * width, 128), width)

    loads[0].wait()
    loads[1].wait()
    loads[2].wait()
    kvall[me] = jnp.dot(x_ref[...], wkv[...], preferred_element_type=F32).astype(BF16)
    got_kv = spread(lambda peer: kvall.at[me], kvall, me, chip, chips, to_chip, s_kv, r_kv)

    def to_other(source, dest, send_sems, recv_sems, i):
        copy = pltpu.make_async_remote_copy(
            src_ref=source, dst_ref=dest, send_sem=send_sems.at[i], recv_sem=recv_sems.at[i],
            device_id={"seq": chip * 2 + other}, device_id_type=MESH,
        )
        copy.start()
        sent.append(copy)
        return copy

    got_pair = [to_other(kvall.at[me], kvall.at[me], s_kv, r_kv, chips - 1)]

    got_g = spread(
        lambda peer: og_hbm.at[:, columns(peer)], gbuf, chip, chip, chips, to_chip, s_g, r_g
    )

    loads[3].wait()
    xbuf[chip] = x_ref[:, columns(chip)]
    gbuf[chip] = og_ref[:, columns(chip)]

    loads[4].wait()
    queries = jnp.dot(x_ref[...], wq[...], preferred_element_type=F32)
    for g in range(heads):
        q3[g] = queries[:, g * head : (g + 1) * head].astype(BF16)
    for k in range(1, chips):
        got_kv[k - 1].wait_recv()
        block = kvall.at[lax.rem(chip + chips - k, chips) * 2 + core]
        got_pair.append(to_other(block, block, s_kv, r_kv, chips - 1 + k))

    loads[5].wait()
    for g in range(heads):
        grad_t = lax.dot_general(
            wo[g * head : (g + 1) * head, :], og_ref[...], NT, preferred_element_type=F32
        )
        dt3[g] = grad_t.astype(BF16)
        d3[g] = grad_t.T.astype(BF16)

    gap = lax.broadcasted_iota(jnp.int32, (tokens, tokens), 0) - lax.broadcasted_iota(
        jnp.int32, (tokens, tokens), 1
    )
    for j in range(n_seq):
        reach = jnp.where(mask_ref[me, j] == 1, jnp.where(me == j, 0, 4 * tokens), -4 * tokens)
        bias[j * tokens : (j + 1) * tokens, :] = jnp.where(gap <= reach, 0.0, -jnp.inf)

    kvacc[...] = jnp.zeros_like(kvacc)
    arrive(got_pair)
    for j in range(n_seq):
        rows = slice(j * tokens, (j + 1) * tokens)
        kt[:, rows] = kvall[j, :, 0:head].astype(F32).T.astype(BF16)
        vt[:, rows] = kvall[j, :, head : 2 * head].astype(F32).T.astype(BF16)

    @pl.loop(0, heads)
    def _(g):
        keys = kvall[:, :, 0:head].reshape(length, head)
        values = kvall[:, :, head : 2 * head].reshape(length, head)
        query = q3[g]
        grad_t = dt3[g]
        scores = lax.dot_general(keys, query, NT, preferred_element_type=F32) * scale + bias[...]
        top = jnp.max(scores, axis=0, keepdims=True)
        raised = jnp.exp(scores - top)
        probs = raised * (1.0 / jnp.sum(raised, axis=0, keepdims=True))
        weights = probs.astype(BF16)
        out_t = jnp.dot(vt[...], weights, preferred_element_type=F32).astype(BF16).astype(F32)
        delta = jnp.sum(grad_t.astype(F32) * out_t, axis=0, keepdims=True)
        prob_grad = jnp.dot(values, grad_t, preferred_element_type=F32)
        score_grad = (probs * (prob_grad - delta)).astype(BF16)
        a3[g] = out_t.T.astype(BF16)
        query_t = jnp.dot(kt[...], score_grad, preferred_element_type=F32) * scale
        qg3[g] = query_t.T.astype(BF16)
        kvacc[:, 0:head] += jnp.dot(score_grad, query, preferred_element_type=F32)
        kvacc[:, head : 2 * head] += jnp.dot(weights, d3[g], preferred_element_type=F32)

    loads[6].wait()
    attn = jnp.concatenate([a3[g] for g in range(heads)], axis=1)
    abuf[chip] = jnp.dot(attn, sel[...], preferred_element_type=F32).astype(BF16)
    got_a = over_chips(abuf, s_a, r_a)
    for g in range(heads):
        qbuf[chip, :, g * head : (g + 1) * head] = qg3[g]
    got_q = over_chips(qbuf, s_q, r_q)
    for j in range(n_seq):
        rows = slice(j * tokens, (j + 1) * tokens)
        kvsend[j % 2, j // 2, :, 0:head] = (kvacc[rows, 0:head] * scale).astype(BF16)
        kvsend[j % 2, j // 2, :, head : 2 * head] = kvacc[rows, head : 2 * head].astype(BF16)
    got_kx = to_other(kvsend.at[other], kvrecv.at[pl.ds(0, chips)], s_kr, r_kr, chips - 1)
    got_x = spread(
        lambda peer: x_hbm.at[:, columns(peer)], xbuf, chip, chip, chips, to_chip, s_x, r_x
    )
    got_kx.wait_recv()
    for c in range(chips):
        rows = pl.ds(pl.multiple_of((c * 2 + core) * tokens, tokens), tokens)
        key_pair = kvacc[rows, 0:head] * scale + kvrecv[c, :, 0:head].astype(F32)
        value_pair = kvacc[rows, head : 2 * head] + kvrecv[c, :, head : 2 * head].astype(F32)
        kvpair[c, :, 0:head] = key_pair.astype(BF16)
        kvpair[c, :, head : 2 * head] = value_pair.astype(BF16)
    got_kr = spread(
        lambda peer: kvpair.at[peer], kvrecv, chips + chip, chip, chips, to_chip, s_kr, r_kr
    )

    arrive(got_g)
    arrive(got_a)
    group = exo_s.shape[1]
    side = n_dp * group
    grads = gbuf[...].reshape(chips * tokens, width)

    def out_rows(which):
        picked = abuf[:, :, pl.ds(pl.multiple_of(which * side, 128), side)]
        return lax.dot_general(
            picked.reshape(chips * tokens, side), grads, TN, preferred_element_type=F32
        )

    theirs = out_rows(other)
    for d in range(n_dp):
        exo_s[d] = theirs[d * group : (d + 1) * group, :].astype(BF16)
    got_exo = swap(exo_s, exo_r, 0)
    part_o[...] = out_rows(core)

    got_exo.wait_recv()
    for d in range(n_dp):
        dpo_s[d] = (part_o[d * group : (d + 1) * group, :] + exo_r[d].astype(F32)).astype(BF16)
    got_do = spread(lambda peer: dpo_s.at[peer], dpo_r, md, md, n_dp, to_dp, s_do, r_do)

    arrive(got_kr)
    own = pl.ds(pl.multiple_of(me * tokens, tokens), tokens)
    key_sum = kvacc[own, 0:head] * scale + kvrecv[chip, :, 0:head].astype(F32)
    value_sum = kvacc[own, head : 2 * head] + kvrecv[chip, :, head : 2 * head].astype(F32)
    for k in range(1, chips):
        peer = chips + lax.rem(chip + k, chips)
        key_sum += kvrecv[peer, :, 0:head].astype(F32)
        value_sum += kvrecv[peer, :, head : 2 * head].astype(F32)
    kgbuf[chip, :, 0:head] = key_sum.astype(BF16)
    kgbuf[chip, :, head : 2 * head] = value_sum.astype(BF16)
    got_kg = over_chips(kgbuf, s_kg, r_kg)

    owned = exq_s.shape[1]

    def rows_of(which, d):
        return pl.ds(pl.multiple_of(which * half + d * owned, 8), owned)

    def projection(grad_buf, part, ex_s, ex_r, i):
        features = xbuf[...].reshape(chips * tokens, width)
        grad = grad_buf[...].reshape(chips * tokens, grad_buf.shape[2])
        part[...] = lax.dot_general(features, grad, TN, preferred_element_type=F32)
        for d in range(n_dp):
            ex_s[d] = part[rows_of(other, d), :].astype(BF16)
        return swap(ex_s, ex_r, i)

    def reduce_dp(got_ex, part, ex_r, dp_s, dp_r, send_sems, recv_sems):
        got_ex.wait_recv()
        for d in range(n_dp):
            dp_s[d] = (part[rows_of(core, d), :] + ex_r[d].astype(F32)).astype(BF16)
        return spread(lambda peer: dp_s.at[peer], dp_r, md, md, n_dp, to_dp, send_sems, recv_sems)

    arrive(got_x)
    arrive(got_q)
    got_exq = projection(qbuf, part_q, exq_s, exq_r, 1)
    got_dq = reduce_dp(got_exq, part_q, exq_r, dpq_s, dpq_r, s_dq, r_dq)

    arrive(got_do)
    mine = pl.ds(pl.multiple_of(md * group, 8), group)
    total = part_o[mine, :] + exo_r[md].astype(F32)
    for k in range(1, n_dp):
        total += dpo_r[lax.rem(md + k, n_dp)].astype(F32)
    padded = group // chips
    for c in range(chips):
        fo_s[c] = total[c * padded : (c + 1) * padded, :].astype(BF16)
    got_fo = spread(lambda peer: fo_s.at[peer], fo_r, chip, chip, chips, to_chip, s_fo, r_fo)
    fo_r[chip] = fo_s[chip]

    arrive(got_kg)
    got_exk = projection(kgbuf, part_k, exk_s, exk_r, 2)
    got_dk = reduce_dp(got_exk, part_k, exk_r, dpk_s, dpk_r, s_dk, r_dk)

    def finish(part, ex_r, dp_r):
        result = part[rows_of(core, md), :] + ex_r[md].astype(F32)
        for k in range(1, n_dp):
            result += dp_r[lax.rem(md + k, n_dp)].astype(F32)
        return result

    q_columns = heads * head
    arrive(got_dq)
    oqkv_ref[:, 0:q_columns] = finish(part_q, exq_r, dpq_r)
    arrive(got_dk)
    oqkv_ref[:, q_columns:] = finish(part_k, exk_r, dpk_r)
    arrive(got_fo)
    for c in range(chips):
        oout_ref[:, c * width : (c + 1) * width] = fo_r[c].astype(F32)[0 : oout_ref.shape[0], :]
    for copy in sent:
        copy.wait_send()


def shards(n_seq, n_dp, layer_input, out_grad, w_query, w_key, w_value, w_output, block_mask):
    tokens, depth = layer_input.shape[1:]
    head = w_key.shape[1]
    q_width = w_query.shape[1]
    heads = q_width // head
    chips = n_seq // 2
    devices = n_seq * n_dp
    width = depth // chips
    rows_in = depth // devices
    rows_out = q_width // devices
    group = chips * round_up(rows_out, 8)
    side = n_dp * group
    length = n_seq * tokens
    selection = jnp.asarray(head_row_selection(n_seq, n_dp, q_width))
    vmem = pltpu.VMEM
    scratch = [
        vmem((tokens, depth), BF16), vmem((tokens, depth), BF16),
        vmem((depth, q_width), BF16), vmem((depth, 2 * head), BF16), vmem((q_width, depth), BF16),
        vmem((q_width, 2 * side), BF16),
        vmem((chips, tokens, width), BF16), vmem((chips, tokens, width), BF16),
        vmem((n_seq, tokens, 2 * head), BF16), vmem((2, chips, tokens, 2 * head), BF16),
        vmem((n_seq, tokens, 2 * head), BF16), vmem((chips, tokens, 2 * head), BF16),
        vmem((length, 2 * head), F32),
        vmem((chips, tokens, 2 * side), BF16), vmem((chips, tokens, q_width), BF16),
        vmem((chips, tokens, 2 * head), BF16),
    ]
    scratch += [vmem((heads, tokens, head), BF16)] * 2 + [vmem((heads, head, tokens), BF16)]
    scratch += [vmem((heads, tokens, head), BF16)] * 2
    scratch += [vmem((head, length), BF16)] * 2 + [vmem((length, tokens), F32)]
    scratch += [vmem((side, width), F32), vmem((width, q_width), F32), vmem((width, 2 * head), F32)]
    out_block = vmem((n_dp, group, width), BF16)
    q_block = vmem((n_dp, rows_in, q_width), BF16)
    k_block = vmem((n_dp, rows_in, 2 * head), BF16)
    scratch += [out_block] * 2 + [q_block] * 2 + [k_block] * 2
    scratch += [out_block] * 2 + [q_block] * 2 + [k_block] * 2
    scratch += [vmem((chips, group // chips, width), BF16)] * 2
    dma = pltpu.SemaphoreType.DMA
    sems = [dma((7,))]
    for count in (chips, chips, n_seq, n_seq, chips, chips, chips, 4, n_dp, n_dp, n_dp, chips):
        sems += [dma((count - 1,))] * 2
    in_vmem = pl.BlockSpec(memory_space=pltpu.VMEM)
    in_hbm = pl.BlockSpec(memory_space=pl.ANY)
    return pl.pallas_call(
        functools.partial(kernel, n_seq, n_dp),
        out_shape=(
            jax.ShapeDtypeStruct((rows_in, q_width + 2 * head), F32),
            jax.ShapeDtypeStruct((rows_out, depth), F32),
        ),
        in_specs=[in_hbm, in_hbm, in_hbm, in_hbm, in_hbm, in_hbm,
                  pl.BlockSpec(memory_space=pltpu.SMEM), in_hbm],
        out_specs=(in_vmem, in_vmem),
        scratch_shapes=scratch + sems,
        compiler_params=pltpu.CompilerParams(
            collective_id=0, has_side_effects=True, vmem_limit_bytes=60 * 1024 * 1024
        ),
    )(layer_input[0], out_grad[0], w_query, w_key, w_value, w_output, block_mask[0], selection)


def solution(mesh):
    placed = (P("dp", "seq", None), P("dp", "seq", None), P(), P(), P(), P(), P("dp", None, None))
    return jax.shard_map(
        functools.partial(shards, mesh.shape["seq"], mesh.shape["dp"]),
        mesh=mesh,
        in_specs=placed,
        out_specs=(P(("seq", "dp"), None), P(("seq", "dp"), None)),
        check_vma=False,
    )
```

```python
import functools
import math

import jax
import jax.numpy as jnp
import ml_dtypes
import numpy as np
from jax import lax
from jax.experimental import pallas as pl
from jax.experimental.pallas import tpu as pltpu
from jax.sharding import PartitionSpec as P

F32 = jnp.float32
BF16 = jnp.bfloat16
MESH = pl.DeviceIdType.MESH
NT = (((1,), (1,)), ((), ()))
TN = (((0,), (0,)), ((), ()))


def round_up(value, step):
    return -(-value // step) * step


def head_row_selection(n_seq, n_dp, width):
    rows = width // (n_seq * n_dp)
    padded = round_up(rows, 8)
    chips = n_seq // 2
    table = np.zeros((width, 2, n_dp, chips, padded), np.float32)
    for core in range(2):
        for d in range(n_dp):
            for c in range(chips):
                for i in range(rows):
                    table[((c * 2 + core) * n_dp + d) * rows + i, core, d, c, i] = 1.0
    return table.reshape(width, -1).astype(ml_dtypes.bfloat16)


def kernel(
    n_seq, n_dp,
    x_hbm, og_hbm, wq_hbm, wk_hbm, wv_hbm, wo_hbm, mask_ref, sel_hbm,
    oqkv_ref, oout_ref,
    x_ref, og_ref, wq, wkv, wo, sel, xbuf, gbuf, kvall, kvsend, kvrecv, kvpair, kvacc, abuf, qbuf, kgbuf,
    q3, d3, dt3, a3, qg3, kt, vt, bias,
    part_o, part_q, part_k,
    exo_s, exo_r, exq_s, exq_r, exk_s, exk_r,
    dpo_s, dpo_r, dpq_s, dpq_r, dpk_s, dpk_r, fo_s, fo_r,
    wsem, s_x, r_x, s_g, r_g, s_kv, r_kv, s_kr, r_kr, s_a, r_a, s_q, r_q, s_kg, r_kg,
    s_ex, r_ex, s_do, r_do, s_dq, r_dq, s_dk, r_dk, s_fo, r_fo,
):
    chips = n_seq // 2
    me = lax.axis_index("seq")
    md = lax.axis_index("dp")
    core = lax.rem(me, 2)
    chip = lax.div(me, 2)
    other = 1 - core
    tokens, depth = x_ref.shape
    heads, _, head = q3.shape
    width = depth // chips
    half = width // 2
    length = n_seq * tokens
    scale = 1.0 / math.sqrt(head)

    loads = [
        pltpu.make_async_copy(wk_hbm, wkv.at[:, 0:head], wsem.at[0]),
        pltpu.make_async_copy(wv_hbm, wkv.at[:, head : 2 * head], wsem.at[1]),
        pltpu.make_async_copy(x_hbm, x_ref, wsem.at[5]),
        pltpu.make_async_copy(og_hbm, og_ref, wsem.at[6]),
        pltpu.make_async_copy(wq_hbm, wq, wsem.at[2]),
        pltpu.make_async_copy(wo_hbm, wo, wsem.at[3]),
        pltpu.make_async_copy(sel_hbm, sel, wsem.at[4]),
    ]
    for load in loads:
        load.start()

    barrier = pltpu.get_barrier_semaphore()
    for k in range(1, n_seq):
        pl.semaphore_signal(
            barrier, inc=1, device_id={"seq": lax.rem(me + k, n_seq)}, device_id_type=MESH
        )
    for k in range(1, n_dp):
        pl.semaphore_signal(
            barrier, inc=1, device_id={"dp": lax.rem(md + k, n_dp)}, device_id_type=MESH
        )
    pl.semaphore_wait(barrier, n_seq + n_dp - 2)

    sent = []

    def spread(source, dest, slot, index, count, to_device, send_sems, recv_sems):
        copies = []
        for k in range(1, count):
            peer = lax.rem(index + k, count)
            copy = pltpu.make_async_remote_copy(
                src_ref=source(peer),
                dst_ref=dest.at[slot],
                send_sem=send_sems.at[k - 1],
                recv_sem=recv_sems.at[k - 1],
                device_id=to_device(peer),
                device_id_type=MESH,
            )
            copy.start()
            copies.append(copy)
        sent.extend(copies)
        return copies

    def to_chip(peer):
        return {"seq": peer * 2 + core}

    def to_dp(peer):
        return {"dp": peer}

    def over_chips(buf, send_sems, recv_sems):
        return spread(
            lambda peer: buf.at[chip], buf, chip, chip, chips, to_chip, send_sems, recv_sems
        )

    def swap(source, dest, i):
        copy = pltpu.make_async_remote_copy(
            src_ref=source, dst_ref=dest, send_sem=s_ex.at[i], recv_sem=r_ex.at[i],
            device_id={"seq": chip * 2 + other}, device_id_type=MESH,
        )
        copy.start()
        sent.append(copy)
        return copy

    def arrive(copies):
        for copy in copies:
            copy.wait_recv()

    def columns(index):
        return pl.ds(pl.multiple_of(index * width, 128), width)

    loads[0].wait()
    loads[1].wait()
    loads[2].wait()
    kvall[me] = jnp.dot(x_ref[...], wkv[...], preferred_element_type=F32).astype(BF16)
    got_kv = spread(lambda peer: kvall.at[me], kvall, me, chip, chips, to_chip, s_kv, r_kv)

    def to_other(source, dest, send_sems, recv_sems, i):
        copy = pltpu.make_async_remote_copy(
            src_ref=source, dst_ref=dest, send_sem=send_sems.at[i], recv_sem=recv_sems.at[i],
            device_id={"seq": chip * 2 + other}, device_id_type=MESH,
        )
        copy.start()
        sent.append(copy)
        return copy

    got_pair = [to_other(kvall.at[me], kvall.at[me], s_kv, r_kv, chips - 1)]

    got_g = spread(
        lambda peer: og_hbm.at[:, columns(peer)], gbuf, chip, chip, chips, to_chip, s_g, r_g
    )

    loads[3].wait()
    xbuf[chip] = x_ref[:, columns(chip)]
    gbuf[chip] = og_ref[:, columns(chip)]

    loads[4].wait()
    queries = jnp.dot(x_ref[...], wq[...], preferred_element_type=F32)
    for g in range(heads):
        q3[g] = queries[:, g * head : (g + 1) * head].astype(BF16)
    for k in range(1, chips):
        got_kv[k - 1].wait_recv()
        block = kvall.at[lax.rem(chip + chips - k, chips) * 2 + core]
        got_pair.append(to_other(block, block, s_kv, r_kv, chips - 1 + k))

    loads[5].wait()
    for g in range(heads):
        grad_t = lax.dot_general(
            wo[g * head : (g + 1) * head, :], og_ref[...], NT, preferred_element_type=F32
        )
        dt3[g] = grad_t.astype(BF16)
        d3[g] = grad_t.T.astype(BF16)

    gap = lax.broadcasted_iota(jnp.int32, (tokens, tokens), 0) - lax.broadcasted_iota(
        jnp.int32, (tokens, tokens), 1
    )
    for j in range(n_seq):
        reach = jnp.where(mask_ref[me, j] == 1, jnp.where(me == j, 0, 4 * tokens), -4 * tokens)
        bias[j * tokens : (j + 1) * tokens, :] = jnp.where(gap <= reach, 0.0, -jnp.inf)

    kvacc[...] = jnp.zeros_like(kvacc)
    arrive(got_pair)
    for j in range(n_seq):
        rows = slice(j * tokens, (j + 1) * tokens)
        kt[:, rows] = kvall[j, :, 0:head].astype(F32).T.astype(BF16)
        vt[:, rows] = kvall[j, :, head : 2 * head].astype(F32).T.astype(BF16)

    @pl.loop(0, heads, unroll=heads)
    def _(g):
        keys = kvall[:, :, 0:head].reshape(length, head)
        values = kvall[:, :, head : 2 * head].reshape(length, head)
        query = q3[g]
        grad_t = dt3[g]
        scores = lax.dot_general(keys, query, NT, preferred_element_type=F32) * scale + bias[...]
        top = jnp.max(scores, axis=0, keepdims=True)
        raised = jnp.exp(scores - top)
        probs = raised * (1.0 / jnp.sum(raised, axis=0, keepdims=True))
        weights = probs.astype(BF16)
        out_t = jnp.dot(vt[...], weights, preferred_element_type=F32).astype(BF16).astype(F32)
        delta = jnp.sum(grad_t.astype(F32) * out_t, axis=0, keepdims=True)
        prob_grad = jnp.dot(values, grad_t, preferred_element_type=F32)
        score_grad = (probs * (prob_grad - delta)).astype(BF16)
        a3[g] = out_t.T.astype(BF16)
        query_t = jnp.dot(kt[...], score_grad, preferred_element_type=F32) * scale
        qg3[g] = query_t.T.astype(BF16)
        kvacc[:, 0:head] += jnp.dot(score_grad, query, preferred_element_type=F32)
        kvacc[:, head : 2 * head] += jnp.dot(weights, d3[g], preferred_element_type=F32)

    loads[6].wait()
    attn = jnp.concatenate([a3[g] for g in range(heads)], axis=1)
    abuf[chip] = jnp.dot(attn, sel[...], preferred_element_type=F32).astype(BF16)
    got_a = over_chips(abuf, s_a, r_a)
    for g in range(heads):
        qbuf[chip, :, g * head : (g + 1) * head] = qg3[g]
    got_q = over_chips(qbuf, s_q, r_q)
    for j in range(n_seq):
        rows = slice(j * tokens, (j + 1) * tokens)
        kvsend[j % 2, j // 2, :, 0:head] = (kvacc[rows, 0:head] * scale).astype(BF16)
        kvsend[j % 2, j // 2, :, head : 2 * head] = kvacc[rows, head : 2 * head].astype(BF16)
    got_kx = to_other(kvsend.at[other], kvrecv.at[pl.ds(0, chips)], s_kr, r_kr, chips - 1)
    got_x = spread(
        lambda peer: x_hbm.at[:, columns(peer)], xbuf, chip, chip, chips, to_chip, s_x, r_x
    )
    got_kx.wait_recv()
    for c in range(chips):
        rows = pl.ds(pl.multiple_of((c * 2 + core) * tokens, tokens), tokens)
        key_pair = kvacc[rows, 0:head] * scale + kvrecv[c, :, 0:head].astype(F32)
        value_pair = kvacc[rows, head : 2 * head] + kvrecv[c, :, head : 2 * head].astype(F32)
        kvpair[c, :, 0:head] = key_pair.astype(BF16)
        kvpair[c, :, head : 2 * head] = value_pair.astype(BF16)
    got_kr = spread(
        lambda peer: kvpair.at[peer], kvrecv, chips + chip, chip, chips, to_chip, s_kr, r_kr
    )

    arrive(got_g)
    arrive(got_a)
    group = exo_s.shape[1]
    side = n_dp * group
    grads = gbuf[...].reshape(chips * tokens, width)

    def out_rows(which):
        picked = abuf[:, :, pl.ds(pl.multiple_of(which * side, 128), side)]
        return lax.dot_general(
            picked.reshape(chips * tokens, side), grads, TN, preferred_element_type=F32
        )

    theirs = out_rows(other)
    for d in range(n_dp):
        exo_s[d] = theirs[d * group : (d + 1) * group, :].astype(BF16)
    got_exo = swap(exo_s, exo_r, 0)
    part_o[...] = out_rows(core)

    got_exo.wait_recv()
    for d in range(n_dp):
        dpo_s[d] = (part_o[d * group : (d + 1) * group, :] + exo_r[d].astype(F32)).astype(BF16)
    got_do = spread(lambda peer: dpo_s.at[peer], dpo_r, md, md, n_dp, to_dp, s_do, r_do)

    arrive(got_kr)
    own = pl.ds(pl.multiple_of(me * tokens, tokens), tokens)
    key_sum = kvacc[own, 0:head] * scale + kvrecv[chip, :, 0:head].astype(F32)
    value_sum = kvacc[own, head : 2 * head] + kvrecv[chip, :, head : 2 * head].astype(F32)
    for k in range(1, chips):
        peer = chips + lax.rem(chip + k, chips)
        key_sum += kvrecv[peer, :, 0:head].astype(F32)
        value_sum += kvrecv[peer, :, head : 2 * head].astype(F32)
    kgbuf[chip, :, 0:head] = key_sum.astype(BF16)
    kgbuf[chip, :, head : 2 * head] = value_sum.astype(BF16)
    got_kg = over_chips(kgbuf, s_kg, r_kg)

    owned = exq_s.shape[1]

    def rows_of(which, d):
        return pl.ds(pl.multiple_of(which * half + d * owned, 8), owned)

    def projection(grad_buf, part, ex_s, ex_r, i):
        features = xbuf[...].reshape(chips * tokens, width)
        grad = grad_buf[...].reshape(chips * tokens, grad_buf.shape[2])
        part[...] = lax.dot_general(features, grad, TN, preferred_element_type=F32)
        for d in range(n_dp):
            ex_s[d] = part[rows_of(other, d), :].astype(BF16)
        return swap(ex_s, ex_r, i)

    def reduce_dp(got_ex, part, ex_r, dp_s, dp_r, send_sems, recv_sems):
        got_ex.wait_recv()
        for d in range(n_dp):
            dp_s[d] = (part[rows_of(core, d), :] + ex_r[d].astype(F32)).astype(BF16)
        return spread(lambda peer: dp_s.at[peer], dp_r, md, md, n_dp, to_dp, send_sems, recv_sems)

    arrive(got_x)
    arrive(got_q)
    got_exq = projection(qbuf, part_q, exq_s, exq_r, 1)
    got_dq = reduce_dp(got_exq, part_q, exq_r, dpq_s, dpq_r, s_dq, r_dq)

    arrive(got_do)
    mine = pl.ds(pl.multiple_of(md * group, 8), group)
    total = part_o[mine, :] + exo_r[md].astype(F32)
    for k in range(1, n_dp):
        total += dpo_r[lax.rem(md + k, n_dp)].astype(F32)
    padded = group // chips
    for c in range(chips):
        fo_s[c] = total[c * padded : (c + 1) * padded, :].astype(BF16)
    got_fo = spread(lambda peer: fo_s.at[peer], fo_r, chip, chip, chips, to_chip, s_fo, r_fo)
    fo_r[chip] = fo_s[chip]

    arrive(got_kg)
    got_exk = projection(kgbuf, part_k, exk_s, exk_r, 2)
    got_dk = reduce_dp(got_exk, part_k, exk_r, dpk_s, dpk_r, s_dk, r_dk)

    def finish(part, ex_r, dp_r):
        result = part[rows_of(core, md), :] + ex_r[md].astype(F32)
        for k in range(1, n_dp):
            result += dp_r[lax.rem(md + k, n_dp)].astype(F32)
        return result

    q_columns = heads * head
    arrive(got_dq)
    oqkv_ref[:, 0:q_columns] = finish(part_q, exq_r, dpq_r)
    arrive(got_dk)
    oqkv_ref[:, q_columns:] = finish(part_k, exk_r, dpk_r)
    arrive(got_fo)
    for c in range(chips):
        oout_ref[:, c * width : (c + 1) * width] = fo_r[c].astype(F32)[0 : oout_ref.shape[0], :]
    for copy in sent:
        copy.wait_send()


def shards(n_seq, n_dp, layer_input, out_grad, w_query, w_key, w_value, w_output, block_mask):
    tokens, depth = layer_input.shape[1:]
    head = w_key.shape[1]
    q_width = w_query.shape[1]
    heads = q_width // head
    chips = n_seq // 2
    devices = n_seq * n_dp
    width = depth // chips
    rows_in = depth // devices
    rows_out = q_width // devices
    group = chips * round_up(rows_out, 8)
    side = n_dp * group
    length = n_seq * tokens
    selection = jnp.asarray(head_row_selection(n_seq, n_dp, q_width))
    vmem = pltpu.VMEM
    scratch = [
        vmem((tokens, depth), BF16), vmem((tokens, depth), BF16),
        vmem((depth, q_width), BF16), vmem((depth, 2 * head), BF16), vmem((q_width, depth), BF16),
        vmem((q_width, 2 * side), BF16),
        vmem((chips, tokens, width), BF16), vmem((chips, tokens, width), BF16),
        vmem((n_seq, tokens, 2 * head), BF16), vmem((2, chips, tokens, 2 * head), BF16),
        vmem((n_seq, tokens, 2 * head), BF16), vmem((chips, tokens, 2 * head), BF16),
        vmem((length, 2 * head), F32),
        vmem((chips, tokens, 2 * side), BF16), vmem((chips, tokens, q_width), BF16),
        vmem((chips, tokens, 2 * head), BF16),
    ]
    scratch += [vmem((heads, tokens, head), BF16)] * 2 + [vmem((heads, head, tokens), BF16)]
    scratch += [vmem((heads, tokens, head), BF16)] * 2
    scratch += [vmem((head, length), BF16)] * 2 + [vmem((length, tokens), F32)]
    scratch += [vmem((side, width), F32), vmem((width, q_width), F32), vmem((width, 2 * head), F32)]
    out_block = vmem((n_dp, group, width), BF16)
    q_block = vmem((n_dp, rows_in, q_width), BF16)
    k_block = vmem((n_dp, rows_in, 2 * head), BF16)
    scratch += [out_block] * 2 + [q_block] * 2 + [k_block] * 2
    scratch += [out_block] * 2 + [q_block] * 2 + [k_block] * 2
    scratch += [vmem((chips, group // chips, width), BF16)] * 2
    dma = pltpu.SemaphoreType.DMA
    sems = [dma((7,))]
    for count in (chips, chips, n_seq, n_seq, chips, chips, chips, 4, n_dp, n_dp, n_dp, chips):
        sems += [dma((count - 1,))] * 2
    in_vmem = pl.BlockSpec(memory_space=pltpu.VMEM)
    in_hbm = pl.BlockSpec(memory_space=pl.ANY)
    return pl.pallas_call(
        functools.partial(kernel, n_seq, n_dp),
        out_shape=(
            jax.ShapeDtypeStruct((rows_in, q_width + 2 * head), F32),
            jax.ShapeDtypeStruct((rows_out, depth), F32),
        ),
        in_specs=[in_hbm, in_hbm, in_hbm, in_hbm, in_hbm, in_hbm,
                  pl.BlockSpec(memory_space=pltpu.SMEM), in_hbm],
        out_specs=(in_vmem, in_vmem),
        scratch_shapes=scratch + sems,
        compiler_params=pltpu.CompilerParams(
            collective_id=0, has_side_effects=True, vmem_limit_bytes=60 * 1024 * 1024
        ),
    )(layer_input[0], out_grad[0], w_query, w_key, w_value, w_output, block_mask[0], selection)


def solution(mesh):
    placed = (P("dp", "seq", None), P("dp", "seq", None), P(), P(), P(), P(), P("dp", None, None))
    return jax.shard_map(
        functools.partial(shards, mesh.shape["seq"], mesh.shape["dp"]),
        mesh=mesh,
        in_specs=placed,
        out_specs=(P(("seq", "dp"), None), P(("seq", "dp"), None)),
        check_vma=False,
    )
```
